32 devices in a mesh: region: 4 (over x, core), sector: 8 (over z, y).
Axes of the slice: x: 2, y: 2, z: 4, core: 2. Of those that a mesh axis runs over, the one named last changes fastest.
Arguments:
- start_state: bfloat16 [4, 32, 128, 4, 128], P('region', 'sector'), may hold values from -6 to 6
- left_env: bfloat16 [4, 32, 16, 128, 128], P('region', 'sector'), may hold values from -0.125 to 0.125
- right_env: bfloat16 [4, 32, 16, 128, 128], P('region', 'sector'), may hold values from -0.5 to 0.5
- mpo_tensor: bfloat16 [16, 4, 4, 16], replicated, may hold values from -0.75 to 0.75
- decay: float32 [4, 32, 128], P('region', 'sector'), may hold values from 0.15 to 1
- energy_terms: float32 [4, 32, 128], P('region', 'sector'), may hold values from -1.2 to 1.2
- live_count: int32 [4, 8], P('region', 'sector'), may hold values from 1 to 4, as said below
Outputs:
- state_out: bfloat16 [4, 32, 128, 4, 128], P('region', 'sector')
- density: float32 [4, 32, 128, 128], P('region', 'sector')
- energy: float32 [4], P('region')
The draws below stay inside these ranges and needn't reach their ends.
Inputs may be any that keep to these rules, and one draw needn't show every extreme that they name: `live_count`: each device's live blocks fill its first slots; some device holds 4 live blocks.
All inputs are finite; a program needn't handle non-finite values.
Results may differ from the reference program's by a relative error of at most 0.0055.
The reference program's roundings to bfloat16 on the way (of `contract_right` and `contract_mpo`) count: a program that leaves them out, or rounds other values in their place, can miss the bound.
Values may be sent and summed in bfloat16 or wider, within the bound.
A program may use at most 64 MiB of HBM per device.

```python
import math
import jax
import jax.numpy as jnp
from jax import lax

BLK = 128
PHYS = 4
CHAN = 16
SLOTS = 4
DAV = 2
LATTICE_PARTS = 4
SECTORS = 8
BLOCKS = 32


def draw_decay(key, part):
    stochastic_seeds = jax.random.split(key, 5)
    array_dimensions = (LATTICE_PARTS, BLOCKS, BLK)
    slow_share = 0.5
    channel_pick = jax.random.uniform(stochastic_seeds[0], (1, BLOCKS, BLK), jnp.float32)
    is_slow = channel_pick < slow_share
    rate_draw = jax.random.uniform(stochastic_seeds[1], (1, BLOCKS, BLK), jnp.float32, 0.2, 1.2)
    tardy_lines = jnp.exp(-rate_draw / LATTICE_PARTS) * jnp.ones(array_dimensions, jnp.float32)
    fast_rows = jax.random.uniform(stochastic_seeds[2], array_dimensions, jnp.float32, 0.3, 0.7)
    spurt_extent = jax.random.uniform(stochastic_seeds[3], array_dimensions, jnp.float32) < 1.5 / LATTICE_PARTS
    spurt_ceiling = jax.random.uniform(stochastic_seeds[4], array_dimensions, jnp.float32, 0.5, 0.8)
    tardy_lines = jnp.where(spurt_extent, tardy_lines * spurt_ceiling, tardy_lines)
    return jnp.where(is_slow, tardy_lines, fast_rows).astype(jnp.float32)


def draw_live_count(key, part):
    stochastic_seeds = jax.random.split(key, 3)
    first_draw = jax.random.randint(stochastic_seeds[0], (LATTICE_PARTS, SECTORS), 0, SLOTS)
    second_draw = jax.random.randint(stochastic_seeds[1], (LATTICE_PARTS, SECTORS), 0, SLOTS)
    counts = 1 + first_draw * second_draw // max(SLOTS - 1, 1)
    chosen = jax.random.randint(stochastic_seeds[2], (), 0, LATTICE_PARTS * SECTORS)
    flat_counts = jnp.where(jnp.arange(LATTICE_PARTS * SECTORS, dtype=jnp.int32) == chosen, SLOTS, counts.reshape(-1))
    return flat_counts.reshape(LATTICE_PARTS, SECTORS).astype(jnp.int32)


def steps_of(rng, extent, cuts, low, largest):
    def one(position, blocks):
        steps = jax.random.uniform(jax.random.fold_in(jax.random.fold_in(rng, 6), position), (blocks,), jnp.float32, low / len(cuts), largest / len(cuts))
        return jnp.repeat(jnp.exp(steps), extent[position] // blocks).reshape((-1,) + (1,) * (len(extent) - position - 1))

    factor_of = one(*cuts[0])
    for cut in cuts[1:]:
        factor_of = factor_of * one(*cut)
    return factor_of


def bell_draw(rng, shape, width, limit, shards=(), kind=jnp.bfloat16):
    array = width * jax.random.normal(rng, shape, jnp.float32)
    if shards:
        array = array * steps_of(rng, shape, shards, -0.22, 0.18)
    return jnp.clip(array, -limit, limit).astype(kind)


def setup_inputs(seed: int = 0) -> dict:
    key_list = jax.random.split(jax.random.key(seed), 8)
    return {
        "start_state": bell_draw(key_list[0], (LATTICE_PARTS, BLOCKS, BLK, PHYS, BLK), 1.0, 6.0, ((0, 4), (1, 8))),
        "left_env": bell_draw(key_list[1], (LATTICE_PARTS, BLOCKS, CHAN, BLK, BLK), (CHAN * BLK) ** -0.5, 0.125, ((0, 4), (1, 8))),
        "right_env": bell_draw(key_list[2], (LATTICE_PARTS, BLOCKS, CHAN, BLK, BLK), BLK ** -0.5, 0.5, ((0, 4), (1, 8))),
        "mpo_tensor": bell_draw(key_list[3], (CHAN, PHYS, PHYS, CHAN), (PHYS * CHAN) ** -0.5, 0.75),
        "decay": draw_decay(jax.random.fold_in(key_list[7], 71), 0),
        "energy_terms": bell_draw(key_list[5], (LATTICE_PARTS, BLOCKS, BLK), 0.2, 1.2, ((0, 4), (1, 8)), jnp.float32),
        "live_count": draw_live_count(jax.random.fold_in(key_list[7], 71), 0),
    }


epsilon = 1e-06

def apply_block(vector, left_part, right_part, mpo_tensor, offset):
    vector_wide = vector.astype(jnp.float32)
    contract_right = jnp.einsum('asc,wcb->aswb', vector_wide, right_part.astype(jnp.float32)).astype(jnp.bfloat16)
    contract_mpo = jnp.einsum('vstw,atwb->asvb', mpo_tensor.astype(jnp.float32), contract_right.astype(jnp.float32)).astype(jnp.bfloat16)
    applied = jnp.einsum('vac,csvb->asb', left_part.astype(jnp.float32), contract_mpo.astype(jnp.float32))
    return applied + offset[:, None, None] * vector_wide

def accumulate(running, row_pair):
    return (row_pair[0] * running + row_pair[1], running)

def reference(start_state, left_env, right_env, mpo_tensor, decay, energy_terms, live_count):
    initial = jnp.zeros((BLOCKS, BLK), jnp.float32)
    unused, offsets = lax.scan(accumulate, initial, (decay, energy_terms))
    scale = math.sqrt(BLOCKS * BLK * PHYS * BLK)

    def region_solve(region_index):
        previous = jnp.maximum(region_index - 1, 0).astype(jnp.int32)
        left_part = lax.dynamic_index_in_dim(left_env, previous, 0, keepdims=False)
        right_part = lax.dynamic_index_in_dim(right_env, region_index, 0, keepdims=False)
        starting = lax.dynamic_index_in_dim(start_state, region_index, 0, keepdims=False)
        offset_rows = lax.dynamic_index_in_dim(offsets, region_index, 0, keepdims=False)
        counts = lax.dynamic_index_in_dim(live_count, region_index, 0, keepdims=False)
        slot_ids = jnp.arange(BLOCKS, dtype=jnp.int32)
        live_mask = slot_ids % SLOTS < counts[slot_ids // SLOTS]

        def operate(vector_bf):

            def count_per_block(block_items):
                vector, left_one, right_one, offset_one, is_active_region = block_items
                return lax.cond(is_active_region, lambda operands: apply_block(operands[0], operands[1], operands[2], mpo_tensor, operands[3]), lambda operands: jnp.zeros(operands[0].shape, jnp.float32), (vector, left_one, right_one, offset_one))
            return lax.map(count_per_block, (vector_bf, left_part, right_part, offset_rows, live_mask))
        first = starting.astype(jnp.float32) * live_mask.astype(jnp.float32)[:, None, None, None]
        norm_sum = jnp.sum(first * first)
        inverse = lax.rsqrt(norm_sum + epsilon)
        current = first * inverse
        applied = operate(first.astype(jnp.bfloat16)) * inverse
        for iteration in range(DAV):
            quotient = jnp.sum(current * applied)
            residual = applied - quotient * current
            resid_sq = jnp.sum(residual * residual)
            factor = lax.rsqrt(resid_sq + epsilon)
            search = residual * factor
            probe_mapped_vector = operate(search.astype(jnp.bfloat16))
            curvature = jnp.sum(search * probe_mapped_vector)
            rotation = 0.5 * jnp.arctan2(-2.0 * resid_sq * factor, curvature - quotient)
            cos_part = jnp.cos(rotation)
            sin_part = jnp.sin(rotation)
            current = cos_part * current + sin_part * search
            applied = cos_part * applied + sin_part * probe_mapped_vector
        energy = jnp.sum(current * applied)
        state_out = (scale * current).astype(jnp.bfloat16)
        state_wide = state_out.astype(jnp.float32)
        density = jnp.einsum('nasb,ncsb->nac', state_wide, state_wide) / (PHYS * BLK)
        return (state_out, density, energy)
    state_out, density, energy = lax.map(region_solve, jnp.arange(LATTICE_PARTS, dtype=jnp.int32))
    return (state_out, density, energy)
```

```python
import functools
import math

import jax
import jax.numpy as jnp
from jax import lax
from jax.experimental import pallas as pl
from jax.experimental.pallas import tpu as pltpu
from jax.sharding import PartitionSpec as P

DAV = 2
EPS = 1e-06
MESH = pl.DeviceIdType.MESH
F32 = jnp.float32
BF16 = jnp.bfloat16
PAD = 8


def half_rotation(y, x):
    top = jnp.maximum(jnp.abs(x), jnp.abs(y))
    safe = jnp.where(top > 0, top, 1.0)
    xn, yn = x / safe, y / safe
    h = jnp.sqrt(xn * xn + yn * yn)
    h = jnp.where(top > 0, h, 1.0)
    big = jnp.sqrt(0.5 * (h + jnp.abs(xn)) / h)
    small = jnp.abs(yn) / (2.0 * h * big)
    big = jnp.where(top > 0, big, 1.0)
    small = jnp.where(top > 0, small, 0.0)
    cos_part = jnp.where(x >= 0, big, small)
    sin_size = jnp.where(x >= 0, small, big)
    return cos_part, jnp.where(y > 0, sin_size, -sin_size)


def kernel(
    regions, sectors, start, left, right, spread, decay, energy, live,
    state_out, density, energy_out,
    left_in, left_t, right_in, right_t, planes, rows_buf, mixed,
    current, applied, search, image, decay_all, energy_all, shift, part, gathered,
    left_send, left_recv, right_sem, own_sem, pre_send, pre_recv, sum_send, sum_recv,
):
    slots, chan, blk, _ = left.shape
    phys = start.shape[1] // blk
    wide = phys * blk
    me, mine = lax.axis_index("region"), lax.axis_index("sector")
    group = 256 // (phys * chan)
    pair = 2 * group
    for n in range(slots):
        pltpu.make_async_copy(right.at[n], right_in.at[n], right_sem.at[n]).start()

    barrier = pltpu.get_barrier_semaphore()
    for k in range(1, regions):
        pl.semaphore_signal(
            barrier, 1, device_id={"region": lax.rem(me + k, regions)}, device_id_type=MESH
        )
    for k in range(1, sectors):
        pl.semaphore_signal(
            barrier, 1, device_id={"sector": lax.rem(mine + k, sectors)}, device_id_type=MESH
        )
    pl.semaphore_wait(barrier, regions + sectors - 2)

    def left_copy(n):
        return pltpu.make_async_remote_copy(
            src_ref=left.at[n], dst_ref=left_in.at[n],
            send_sem=left_send.at[n], recv_sem=left_recv.at[n],
            device_id={"region": lax.rem(me + 1, regions)}, device_id_type=MESH,
        )

    def own_copy(n):
        return pltpu.make_async_copy(left.at[n], left_in.at[n], own_sem.at[n])

    def prefix_copies(k, slot):
        to = {"region": lax.rem(me + k, regions)}
        return [
            pltpu.make_async_remote_copy(
                src_ref=src, dst_ref=dst.at[slot],
                send_sem=pre_send.at[i, k - 1], recv_sem=pre_recv.at[i, k - 1],
                device_id=to, device_id_type=MESH,
            )
            for i, (src, dst) in enumerate(((decay, decay_all), (energy, energy_all)))
        ]

    for k in range(1, regions):
        for copy in prefix_copies(k, me):
            copy.start()

    @pl.when(me < regions - 1)
    def _():
        for n in range(slots):
            left_copy(n).start()

    @pl.when(me == 0)
    def _():
        for n in range(slots):
            own_copy(n).start()

    decay_all[me] = decay[...]
    energy_all[me] = energy[...]
    for k in range(1, regions):
        for copy in prefix_copies(k, lax.rem(me + regions - k, regions)):
            copy.wait()
    offsets = jnp.zeros((slots, blk), F32)
    for p in range(regions - 1):
        offsets = jnp.where(p < me, decay_all[p] * offsets + energy_all[p], offsets)
    shift[...] = offsets

    live_slots = live[0, 0]

    def prepare_right(n):
        pltpu.make_async_copy(right.at[n], right_in.at[n], right_sem.at[n]).wait()
        pitch = blk + PAD
        for w in range(chan):
            planes[w * pitch : w * pitch + blk, :] = right_in[n, w].astype(F32).T
        for b in range(blk):
            right_t[n, b * chan : (b + 1) * chan, :] = planes[
                pl.ds(b, chan, stride=pitch), :
            ].astype(BF16)

    def prepare_left(n):
        for u in range(chan):
            left_t[n, u * blk : (u + 1) * blk, :] = left_in[n, u].T

    def sum8(value):
        return jnp.sum(value.reshape(-1, 8, value.shape[-1]), axis=0)

    def operate(n, vector, arrive):
        for j in range(blk // pair):
            rows = right_t[n, j * pair * chan : (j + 1) * pair * chan, :]
            first = jnp.dot(rows, vector, preferred_element_type=F32).astype(BF16)
            half = group * chan
            stacked = [
                jnp.concatenate(
                    [
                        first[g * half : (g + 1) * half, t * blk : (t + 1) * blk]
                        for t in range(phys)
                    ],
                    axis=0,
                )
                for g in range(2)
            ]
            second = jnp.dot(
                spread[...], jnp.concatenate(stacked, axis=1), preferred_element_type=F32
            ).astype(BF16)
            tile = group * phys
            for g in range(2):
                row = (2 * j + g) * tile
                for u in range(chan):
                    mixed[row : row + tile, u * blk : (u + 1) * blk] = second[
                        u * tile : (u + 1) * tile, g * blk : (g + 1) * blk
                    ]
        arrive()
        rows_buf[...] = jnp.dot(mixed[...], left_t[n], preferred_element_type=F32)
        return [rows_buf[pl.ds(s, blk, stride=phys), :] for s in range(phys)]

    def reduce(turn, sums):
        lines = lax.broadcasted_iota(jnp.int32, (8, blk), 0)
        tile = jnp.zeros((8, blk), F32)
        for q, total in enumerate(sums):
            tile = jnp.where(lines == q, jnp.sum(total, axis=0, keepdims=True), tile)
        part[turn] = tile
        gathered[turn, mine] = tile

        def copy_of(k, slot):
            return pltpu.make_async_remote_copy(
                src_ref=part.at[turn], dst_ref=gathered.at[turn, slot],
                send_sem=sum_send.at[turn, k - 1], recv_sem=sum_recv.at[turn, k - 1],
                device_id={"sector": lax.rem(mine + k, sectors)}, device_id_type=MESH,
            )

        for k in range(1, sectors):
            copy_of(k, mine).start()
        for k in range(1, sectors):
            copy_of(k, lax.rem(mine + sectors - k, sectors)).wait()
        total = gathered[turn, 0]
        for i in range(1, sectors):
            total = total + gathered[turn, i]
        total = jnp.broadcast_to(jnp.sum(total, axis=1, keepdims=True), (8, blk))
        return [total[q : q + 1] for q in range(len(sums))]

    zero = jnp.zeros((8, blk), F32)

    def open_slot(n, sums):
        prepare_right(n)
        alive = jnp.where(n < live_slots, 1.0, 0.0).astype(F32)
        rows_buf[...] = start[n].astype(F32)
        firsts = []
        for t in range(phys):
            first = rows_buf[pl.ds(t, blk, stride=phys), :].T * alive
            current[n, t] = first
            firsts.append(first.astype(BF16))
        offset = shift[pl.ds(n, 1)]

        def arrive():
            @pl.when(me > 0)
            def _():
                left_copy(n).wait_recv()

            @pl.when(me == 0)
            def _():
                own_copy(n).wait()

            prepare_left(n)

        results = operate(n, jnp.concatenate(firsts, axis=1), arrive)
        a, b, c = sums
        for s in range(phys):
            first = current[n, s]
            value = results[s] + offset * first
            applied[n, s] = value
            a, b, c = a + sum8(first * first), b + sum8(first * value), c + sum8(value * value)
        return a, b, c

    sums = lax.fori_loop(0, slots, open_slot, (zero, zero, zero))
    norm_sum, first_quotient, first_sq = reduce(0, sums)
    inverse = lax.rsqrt(norm_sum + EPS)
    quotient = first_quotient * inverse * inverse
    image_sq = first_sq * inverse * inverse
    weight = norm_sum / (norm_sum + EPS)
    cos_part = inverse
    sin_part = None
    for turn in range(DAV):
        resid_sq = image_sq - quotient * quotient * (2.0 - weight)
        factor = lax.rsqrt(resid_sq + EPS)

        def next_slot(n, sums, cos_part=cos_part, sin_part=sin_part, quotient=quotient, factor=factor):
            probes = []
            for t in range(phys):
                state, moved = cos_part * current[n, t], cos_part * applied[n, t]
                if sin_part is not None:
                    state = state + sin_part * search[n, t]
                    moved = moved + sin_part * image[n, t]
                current[n, t] = state
                applied[n, t] = moved
                probe = (moved - quotient * state) * factor
                search[n, t] = probe
                probes.append(probe.astype(BF16))
            results = operate(n, jnp.concatenate(probes, axis=1), lambda: None)
            offset = shift[pl.ds(n, 1)]
            a, b, c = sums
            for s in range(phys):
                value = results[s] + offset * search[n, s].astype(BF16).astype(F32)
                image[n, s] = value
                a = a + sum8(current[n, s] * value)
                b = b + sum8(applied[n, s] * value)
                c = c + sum8(value * value)
            return a, b, c

        sums = lax.fori_loop(0, slots, next_slot, (zero, zero, zero))
        along_state, along_image, search_sq = reduce(turn + 1, sums)
        curvature = factor * (along_image - quotient * along_state)
        cos_part, sin_part = half_rotation(-2.0 * resid_sq * factor, curvature - quotient)
        cross_term = factor * (image_sq - quotient * quotient)
        inner_term = factor * quotient * (1.0 - weight)
        next_quotient = (
            cos_part * cos_part * quotient
            + cos_part * sin_part * (along_state + cross_term)
            + sin_part * sin_part * curvature
        )
        next_sq = (
            cos_part * cos_part * image_sq
            + 2.0 * cos_part * sin_part * along_image
            + sin_part * sin_part * search_sq
        )
        weight = (
            cos_part * cos_part * weight
            + 2.0 * cos_part * sin_part * inner_term
            + sin_part * sin_part * resid_sq * factor * factor
        )
        quotient, image_sq = next_quotient, next_sq

    energy_out[0] = quotient[0, 0]
    scale = math.sqrt(slots * sectors * blk * phys * blk)

    def close_slot(n, carry):
        total = jnp.zeros((blk, blk), F32)
        for s in range(phys):
            state = scale * (cos_part * current[n, s] + sin_part * search[n, s])
            turned = state.T
            rows_buf[pl.ds(s, blk, stride=phys), :] = turned
            total = total + jnp.dot(
                turned.astype(BF16), state.astype(BF16), preferred_element_type=F32
            )
        state_out[n] = rows_buf[...].astype(BF16)
        density[n] = total / (phys * blk)
        return carry

    lax.fori_loop(0, slots, close_slot, 0)

    @pl.when(me < regions - 1)
    def _():
        for n in range(slots):
            left_copy(n).wait_send()


def body(regions, sectors, start_state, left_env, right_env, mpo_tensor, decay, energy_terms, live_count):
    _, slots, blk, phys, _ = start_state.shape
    chan = left_env.shape[2]
    wide = phys * blk
    group = 256 // (phys * chan)
    spread = jnp.einsum(
        "ustw,gh->ugsthw", mpo_tensor, jnp.eye(group, dtype=mpo_tensor.dtype)
    ).reshape(chan * group * phys, phys * group * chan)
    vmem = pl.BlockSpec(memory_space=pltpu.VMEM)
    hbm = pl.BlockSpec(memory_space=pl.ANY)
    smem = pl.BlockSpec(memory_space=pltpu.SMEM)
    dma = pltpu.SemaphoreType.DMA
    state = pltpu.VMEM((slots, phys, blk, blk), F32)
    outs = pl.pallas_call(
        functools.partial(kernel, regions, sectors),
        out_shape=(
            jax.ShapeDtypeStruct((slots, wide, blk), BF16),
            jax.ShapeDtypeStruct((slots, blk, blk), F32),
            jax.ShapeDtypeStruct((1,), F32),
        ),
        in_specs=[vmem, hbm, hbm, vmem, vmem, vmem, smem],
        out_specs=(vmem, vmem, smem),
        scratch_shapes=[
            pltpu.VMEM((slots, chan, blk, blk), BF16),
            pltpu.VMEM((slots, chan * blk, blk), BF16),
            pltpu.VMEM((slots, chan, blk, blk), BF16),
            pltpu.VMEM((slots, chan * blk, blk), BF16),
            pltpu.VMEM((chan * (blk + PAD), blk), F32),
            pltpu.VMEM((wide, blk), F32),
            pltpu.VMEM((wide, chan * blk), BF16),
            state, state, state, state,
            pltpu.VMEM((regions, slots, blk), F32),
            pltpu.VMEM((regions, slots, blk), F32),
            pltpu.VMEM((slots, blk), F32),
            pltpu.VMEM((DAV + 1, 8, blk), F32),
            pltpu.VMEM((DAV + 1, sectors, 8, blk), F32),
            dma((slots,)), dma((slots,)), dma((slots,)), dma((slots,)),
            dma((2, regions)), dma((2, regions)),
            dma((DAV + 1, sectors)), dma((DAV + 1, sectors)),
        ],
        compiler_params=pltpu.CompilerParams(collective_id=0, has_side_effects=True),
    )(
        start_state.reshape(slots, wide, blk), left_env[0], right_env[0], spread,
        decay[0], energy_terms[0], live_count,
    )
    return (
        outs[0].reshape(start_state.shape),
        outs[1].reshape(1, slots, blk, blk),
        outs[2],
    )


def solution(mesh):
    in_specs = (
        P("region", "sector", None, None, None),
        P("region", "sector", None, None, None),
        P("region", "sector", None, None, None),
        P(),
        P("region", "sector", None),
        P("region", "sector", None),
        P("region", "sector"),
    )
    out_specs = (
        P("region", "sector", None, None, None),
        P("region", "sector", None, None),
        P("region"),
    )
    step = functools.partial(body, mesh.shape["region"], mesh.shape["sector"])
    return jax.shard_map(step, mesh=mesh, in_specs=in_specs, out_specs=out_specs, check_vma=False)
```

```python
import functools
import math

import jax
import jax.numpy as jnp
from jax import lax
from jax.experimental import pallas as pl
from jax.experimental.pallas import tpu as pltpu
from jax.sharding import PartitionSpec as P

DAV = 2
EPS = 1e-06
MESH = pl.DeviceIdType.MESH
F32 = jnp.float32
BF16 = jnp.bfloat16
PAD = 8


def half_rotation(y, x):
    top = jnp.maximum(jnp.abs(x), jnp.abs(y))
    safe = jnp.where(top > 0, top, 1.0)
    xn, yn = x / safe, y / safe
    h = jnp.sqrt(xn * xn + yn * yn)
    h = jnp.where(top > 0, h, 1.0)
    big = jnp.sqrt(0.5 * (h + jnp.abs(xn)) / h)
    small = jnp.abs(yn) / (2.0 * h * big)
    big = jnp.where(top > 0, big, 1.0)
    small = jnp.where(top > 0, small, 0.0)
    cos_part = jnp.where(x >= 0, big, small)
    sin_size = jnp.where(x >= 0, small, big)
    return cos_part, jnp.where(y > 0, sin_size, -sin_size)


def kernel(
    regions, sectors, start, left, right, operator, decay, energy, live,
    state_out, energy_out,
    start_in, left_in, left_t, right_in, right_t, planes, rows_buf, mixed, lines, spread,
    current, applied, search, image, decay_all, energy_all, shift, part, gathered,
    left_send, left_recv, right_sem, own_sem, start_sem, pre_send, pre_recv, sum_send, sum_recv,
):
    slots, chan, blk, _ = left.shape
    phys = start.shape[1] // blk
    wide = phys * blk
    me, mine = lax.axis_index("region"), lax.axis_index("sector")
    group = 256 // (phys * chan)
    pair = 2 * group
    for n in range(slots):
        pltpu.make_async_copy(right.at[n], right_in.at[n], right_sem.at[n]).start()
        pltpu.make_async_copy(start.at[n], start_in.at[n], start_sem.at[n]).start()

    barrier = pltpu.get_barrier_semaphore()
    for k in range(1, regions):
        pl.semaphore_signal(
            barrier, 1, device_id={"region": lax.rem(me + k, regions)}, device_id_type=MESH
        )
    for k in range(1, sectors):
        pl.semaphore_signal(
            barrier, 1, device_id={"sector": lax.rem(mine + k, sectors)}, device_id_type=MESH
        )
    pl.semaphore_wait(barrier, regions + sectors - 2)

    def left_copy(n):
        return pltpu.make_async_remote_copy(
            src_ref=left.at[n], dst_ref=left_in.at[n],
            send_sem=left_send.at[n], recv_sem=left_recv.at[n],
            device_id={"region": lax.rem(me + 1, regions)}, device_id_type=MESH,
        )

    def own_copy(n):
        return pltpu.make_async_copy(left.at[n], left_in.at[n], own_sem.at[n])

    def prefix_copies(k, slot):
        to = {"region": lax.rem(me + k, regions)}
        return [
            pltpu.make_async_remote_copy(
                src_ref=src, dst_ref=dst.at[slot],
                send_sem=pre_send.at[i, k - 1], recv_sem=pre_recv.at[i, k - 1],
                device_id=to, device_id_type=MESH,
            )
            for i, (src, dst) in enumerate(((decay, decay_all), (energy, energy_all)))
        ]

    for k in range(1, regions):
        for copy in prefix_copies(k, me):
            copy.start()

    @pl.when(me < regions - 1)
    def _():
        for n in range(slots):
            left_copy(n).start()

    @pl.when(me == 0)
    def _():
        for n in range(slots):
            own_copy(n).start()

    decay_all[me] = decay[...]
    energy_all[me] = energy[...]
    for k in range(1, regions):
        for copy in prefix_copies(k, lax.rem(me + regions - k, regions)):
            copy.wait()
    offsets = jnp.zeros((slots, blk), F32)
    for p in range(regions - 1):
        offsets = jnp.where(p < me, decay_all[p] * offsets + energy_all[p], offsets)
    shift[...] = offsets

    live_slots = live[0, 0]

    side = group * phys * chan
    lines[...] = operator[...].astype(F32)

    def where_one(test):
        return jnp.where(test, 1.0, 0.0).astype(BF16)

    def grid_of(shape):
        return [lax.broadcasted_iota(jnp.int32, shape, i) for i in range(2)]

    r, c = grid_of((side, chan * phys))
    pick_row = where_one((r // (group * phys) == c // phys) & (r % phys == c % phys))
    r, c = grid_of((chan, side))
    total = jnp.zeros((side, side), F32)
    for t in range(phys):
        tall = jnp.dot(
            pick_row,
            lines[pl.ds(t, chan * phys, stride=phys), :].astype(BF16),
            preferred_element_type=F32,
        ).astype(BF16)
        pick_column = where_one((c // (group * chan) == t) & (c % chan == r))
        total = total + jnp.dot(tall, pick_column, preferred_element_type=F32)
    r, c = grid_of((side, side))
    same = (r // phys) % group == (c // chan) % group
    spread[...] = jnp.where(same, total, 0.0).astype(BF16)

    def prepare_right(n):
        pltpu.make_async_copy(right.at[n], right_in.at[n], right_sem.at[n]).wait()
        pitch = blk + PAD
        for w in range(chan):
            planes[w * pitch : w * pitch + blk, :] = right_in[n, w].astype(F32).T
        for b in range(blk):
            right_t[n, b * chan : (b + 1) * chan, :] = planes[
                pl.ds(b, chan, stride=pitch), :
            ].astype(BF16)

    def prepare_left(n):
        for u in range(chan):
            left_t[n, u * blk : (u + 1) * blk, :] = left_in[n, u].T

    def sum8(value):
        return jnp.sum(value.reshape(-1, 8, value.shape[-1]), axis=0)

    def operate(n, slot, vector, arrive):
        half = group * chan
        for j in range(blk // pair):
            rows = right_t[n, j * pair * chan : (j + 1) * pair * chan, :]
            first = jnp.dot(rows, vector, preferred_element_type=F32).astype(BF16)
            stacked = [
                jnp.concatenate(
                    [
                        first[g * half : (g + 1) * half, t * blk : (t + 1) * blk]
                        for t in range(phys)
                    ],
                    axis=0,
                )
                for g in range(2)
            ]
            second = jnp.dot(
                spread[...], jnp.concatenate(stacked, axis=1), preferred_element_type=F32
            ).astype(BF16)
            tile = group * phys
            for g in range(2):
                row = (2 * j + g) * tile
                for u in range(chan):
                    mixed[slot, row : row + tile, u * blk : (u + 1) * blk] = second[
                        u * tile : (u + 1) * tile, g * blk : (g + 1) * blk
                    ]
        arrive()
        rows_buf[slot] = jnp.dot(mixed[slot], left_t[n], preferred_element_type=F32)
        return [rows_buf[slot, pl.ds(s, blk, stride=phys), :] for s in range(phys)]

    def reduce(turn, sums):
        line = lax.broadcasted_iota(jnp.int32, (8, blk), 0)
        tile = jnp.zeros((8, blk), F32)
        for q, total in enumerate(sums):
            tile = jnp.where(line == q, jnp.sum(total, axis=0, keepdims=True), tile)
        part[turn] = tile
        gathered[turn, mine] = tile

        def copy_of(k, slot):
            return pltpu.make_async_remote_copy(
                src_ref=part.at[turn], dst_ref=gathered.at[turn, slot],
                send_sem=sum_send.at[turn, k - 1], recv_sem=sum_recv.at[turn, k - 1],
                device_id={"sector": lax.rem(mine + k, sectors)}, device_id_type=MESH,
            )

        for k in range(1, sectors):
            copy_of(k, mine).start()
        for k in range(1, sectors):
            copy_of(k, lax.rem(mine + sectors - k, sectors)).wait()
        total = gathered[turn, 0]
        for i in range(1, sectors):
            total = total + gathered[turn, i]
        total = jnp.broadcast_to(jnp.sum(total, axis=1, keepdims=True), (8, blk))
        return [total[q : q + 1] for q in range(len(sums))]

    zero = jnp.zeros((8, blk), F32)

    def open_slot(n, sums):
        prepare_right(n)
        alive = jnp.where(n < live_slots, 1.0, 0.0).astype(F32)
        pltpu.make_async_copy(start.at[n], start_in.at[n], start_sem.at[n]).wait()
        rows_buf[0] = start_in[n].astype(F32)
        firsts = []
        for t in range(phys):
            first = rows_buf[0, pl.ds(t, blk, stride=phys), :].T * alive
            current[n, t] = first
            firsts.append(first.astype(BF16))
        offset = shift[pl.ds(n, 1)]

        def arrive():
            @pl.when(me > 0)
            def _():
                left_copy(n).wait_recv()

            @pl.when(me == 0)
            def _():
                own_copy(n).wait()

            prepare_left(n)

        results = operate(n, 0, jnp.concatenate(firsts, axis=1), arrive)
        a, b, c = sums
        for s in range(phys):
            first = current[n, s]
            value = results[s] + offset * first
            applied[n, s] = value
            a, b, c = a + sum8(first * first), b + sum8(first * value), c + sum8(value * value)
        return a, b, c

    sums = lax.fori_loop(0, slots, open_slot, (zero, zero, zero))
    norm_sum, first_quotient, first_sq = reduce(0, sums)
    inverse = lax.rsqrt(norm_sum + EPS)
    quotient = first_quotient * inverse * inverse
    image_sq = first_sq * inverse * inverse
    weight = norm_sum / (norm_sum + EPS)
    cos_part = inverse
    sin_part = None
    for turn in range(DAV):
        resid_sq = image_sq - quotient * quotient * (2.0 - weight)
        factor = lax.rsqrt(resid_sq + EPS)

        def next_slot(n, sums, cos_part=cos_part, sin_part=sin_part, quotient=quotient, factor=factor):
            probes = []
            for t in range(phys):
                state, moved = cos_part * current[n, t], cos_part * applied[n, t]
                if sin_part is not None:
                    state = state + sin_part * search[n, t]
                    moved = moved + sin_part * image[n, t]
                current[n, t] = state
                applied[n, t] = moved
                probe = (moved - quotient * state) * factor
                search[n, t] = probe
                probes.append(probe.astype(BF16))
            results = operate(n, 0, jnp.concatenate(probes, axis=1), lambda: None)
            offset = shift[pl.ds(n, 1)]
            a, b, c = sums
            for s in range(phys):
                value = results[s] + offset * search[n, s].astype(BF16).astype(F32)
                image[n, s] = value
                a = a + sum8(current[n, s] * value)
                b = b + sum8(applied[n, s] * value)
                c = c + sum8(value * value)
            return a, b, c

        sums = lax.fori_loop(0, slots, next_slot, (zero, zero, zero))
        along_state, along_image, search_sq = reduce(turn + 1, sums)
        curvature = factor * (along_image - quotient * along_state)
        cos_part, sin_part = half_rotation(-2.0 * resid_sq * factor, curvature - quotient)
        cross_term = factor * (image_sq - quotient * quotient)
        inner_term = factor * quotient * (1.0 - weight)
        next_quotient = (
            cos_part * cos_part * quotient
            + cos_part * sin_part * (along_state + cross_term)
            + sin_part * sin_part * curvature
        )
        next_sq = (
            cos_part * cos_part * image_sq
            + 2.0 * cos_part * sin_part * along_image
            + sin_part * sin_part * search_sq
        )
        weight = (
            cos_part * cos_part * weight
            + 2.0 * cos_part * sin_part * inner_term
            + sin_part * sin_part * resid_sq * factor * factor
        )
        quotient, image_sq = next_quotient, next_sq

    energy_out[0] = quotient[0, 0]
    scale = math.sqrt(slots * sectors * blk * phys * blk)

    for n in range(slots):
        for t in range(phys):
            state = cos_part * current[n, t] + sin_part * search[n, t]
            state_out[n, t] = (scale * state).astype(BF16)

    @pl.when(me < regions - 1)
    def _():
        for n in range(slots):
            left_copy(n).wait_send()


def finish(state, out, density, rows_buf):
    _, phys, blk, _ = state.shape
    total = jnp.zeros((blk, blk), F32)
    for s in range(phys):
        turned = state[0, s].T
        rows_buf[pl.ds(s, blk, stride=phys), :] = turned.astype(F32)
        total = total + jnp.dot(turned, state[0, s], preferred_element_type=F32)
    out[0] = rows_buf[...].astype(BF16)
    density[0] = total / (phys * blk)


def body(regions, sectors, start_state, left_env, right_env, mpo_tensor, decay, energy_terms, live_count):
    _, slots, blk, phys, _ = start_state.shape
    chan = left_env.shape[2]
    wide = phys * blk
    group = 256 // (phys * chan)
    vmem = pl.BlockSpec(memory_space=pltpu.VMEM)
    hbm = pl.BlockSpec(memory_space=pl.ANY)
    smem = pl.BlockSpec(memory_space=pltpu.SMEM)
    dma = pltpu.SemaphoreType.DMA
    state = pltpu.VMEM((slots, phys, blk, blk), F32)
    outs = pl.pallas_call(
        functools.partial(kernel, regions, sectors),
        out_shape=(
            jax.ShapeDtypeStruct((slots, phys, blk, blk), BF16),
            jax.ShapeDtypeStruct((1,), F32),
        ),
        in_specs=[hbm, hbm, hbm, vmem, vmem, vmem, smem],
        out_specs=(vmem, smem),
        scratch_shapes=[
            pltpu.VMEM((slots, wide, blk), BF16),
            pltpu.VMEM((slots, chan, blk, blk), BF16),
            pltpu.VMEM((slots, chan * blk, blk), BF16),
            pltpu.VMEM((slots, chan, blk, blk), BF16),
            pltpu.VMEM((slots, chan * blk, blk), BF16),
            pltpu.VMEM((chan * (blk + PAD), blk), F32),
            pltpu.VMEM((2, wide, blk), F32),
            pltpu.VMEM((2, wide, chan * blk), BF16),
            pltpu.VMEM((chan * phys * phys, chan), F32),
            pltpu.VMEM((group * phys * chan, group * phys * chan), BF16),
            state, state, state, state,
            pltpu.VMEM((regions, slots, blk), F32),
            pltpu.VMEM((regions, slots, blk), F32),
            pltpu.VMEM((slots, blk), F32),
            pltpu.VMEM((DAV + 1, 8, blk), F32),
            pltpu.VMEM((DAV + 1, sectors, 8, blk), F32),
            dma((slots,)), dma((slots,)), dma((slots,)), dma((slots,)), dma((slots,)),
            dma((2, regions)), dma((2, regions)),
            dma((DAV + 1, sectors)), dma((DAV + 1, sectors)),
        ],
        compiler_params=pltpu.CompilerParams(collective_id=0, has_side_effects=True),
    )(
        start_state.reshape(slots, wide, blk), left_env[0], right_env[0],
        mpo_tensor.reshape(chan * phys * phys, chan),
        decay[0], energy_terms[0], live_count,
    )
    state_out, density = pl.pallas_call(
        finish,
        grid=(slots,),
        out_shape=(
            jax.ShapeDtypeStruct((slots, wide, blk), BF16),
            jax.ShapeDtypeStruct((slots, blk, blk), F32),
        ),
        in_specs=[pl.BlockSpec((1, phys, blk, blk), lambda n: (n, 0, 0, 0))],
        out_specs=(
            pl.BlockSpec((1, wide, blk), lambda n: (n, 0, 0)),
            pl.BlockSpec((1, blk, blk), lambda n: (n, 0, 0)),
        ),
        scratch_shapes=[pltpu.VMEM((wide, blk), F32)],
    )(outs[0])
    return (
        state_out.reshape(start_state.shape),
        density.reshape(1, slots, blk, blk),
        outs[1],
    )


def solution(mesh):
    in_specs = (
        P("region", "sector", None, None, None),
        P("region", "sector", None, None, None),
        P("region", "sector", None, None, None),
        P(),
        P("region", "sector", None),
        P("region", "sector", None),
        P("region", "sector"),
    )
    out_specs = (
        P("region", "sector", None, None, None),
        P("region", "sector", None, None),
        P("region"),
    )
    step = functools.partial(body, mesh.shape["region"], mesh.shape["sector"])
    return jax.shard_map(step, mesh=mesh, in_specs=in_specs, out_specs=out_specs, check_vma=False)
```

```python
import functools
import math

import jax
import jax.numpy as jnp
from jax import lax
from jax.experimental import pallas as pl
from jax.experimental.pallas import tpu as pltpu
from jax.sharding import PartitionSpec as P

DAV = 2
EPS = 1e-06
MESH = pl.DeviceIdType.MESH
F32 = jnp.float32
BF16 = jnp.bfloat16
PAD = 8


def half_rotation(y, x):
    top = jnp.maximum(jnp.abs(x), jnp.abs(y))
    safe = jnp.where(top > 0, top, 1.0)
    xn, yn = x / safe, y / safe
    h = jnp.sqrt(xn * xn + yn * yn)
    h = jnp.where(top > 0, h, 1.0)
    big = jnp.sqrt(0.5 * (h + jnp.abs(xn)) / h)
    small = jnp.abs(yn) / (2.0 * h * big)
    big = jnp.where(top > 0, big, 1.0)
    small = jnp.where(top > 0, small, 0.0)
    cos_part = jnp.where(x >= 0, big, small)
    sin_size = jnp.where(x >= 0, small, big)
    return cos_part, jnp.where(y > 0, sin_size, -sin_size)


def kernel(
    regions, sectors, start, left, right, operator, decay, energy, live,
    state_out, energy_out,
    start_in, left_in, left_t, right_in, right_t, planes, rows_buf, mixed, lines, spread,
    current, applied, search, image, decay_all, energy_all, shift, part, gathered,
    left_send, left_recv, right_sem, own_sem, start_sem, pre_send, pre_recv, sum_send, sum_recv,
):
    slots, chan, blk, _ = left.shape
    phys = start.shape[1] // blk
    wide = phys * blk
    me, mine = lax.axis_index("region"), lax.axis_index("sector")
    group = 256 // (phys * chan)
    pair = 2 * group
    for n in range(slots):
        pltpu.make_async_copy(right.at[n], right_in.at[n], right_sem.at[n]).start()
        pltpu.make_async_copy(start.at[n], start_in.at[n], start_sem.at[n]).start()

    barrier = pltpu.get_barrier_semaphore()
    for k in range(1, regions):
        pl.semaphore_signal(
            barrier, 1, device_id={"region": lax.rem(me + k, regions)}, device_id_type=MESH
        )
    for k in range(1, sectors):
        pl.semaphore_signal(
            barrier, 1, device_id={"sector": lax.rem(mine + k, sectors)}, device_id_type=MESH
        )
    pl.semaphore_wait(barrier, regions + sectors - 2)

    def left_copy(n):
        return pltpu.make_async_remote_copy(
            src_ref=left.at[n], dst_ref=left_in.at[n],
            send_sem=left_send.at[n], recv_sem=left_recv.at[n],
            device_id={"region": lax.rem(me + 1, regions)}, device_id_type=MESH,
        )

    def own_copy(n):
        return pltpu.make_async_copy(left.at[n], left_in.at[n], own_sem.at[n])

    def prefix_copies(k, slot):
        to = {"region": lax.rem(me + k, regions)}
        return [
            pltpu.make_async_remote_copy(
                src_ref=src, dst_ref=dst.at[slot],
                send_sem=pre_send.at[i, k - 1], recv_sem=pre_recv.at[i, k - 1],
                device_id=to, device_id_type=MESH,
            )
            for i, (src, dst) in enumerate(((decay, decay_all), (energy, energy_all)))
        ]

    for k in range(1, regions):
        for copy in prefix_copies(k, me):
            copy.start()

    @pl.when(me < regions - 1)
    def _():
        for n in range(slots):
            left_copy(n).start()

    @pl.when(me == 0)
    def _():
        for n in range(slots):
            own_copy(n).start()

    decay_all[me] = decay[...]
    energy_all[me] = energy[...]
    for k in range(1, regions):
        for copy in prefix_copies(k, lax.rem(me + regions - k, regions)):
            copy.wait()
    offsets = jnp.zeros((slots, blk), F32)
    for p in range(regions - 1):
        offsets = jnp.where(p < me, decay_all[p] * offsets + energy_all[p], offsets)
    shift[...] = offsets

    live_slots = live[...]

    side = group * phys * chan
    lines[...] = operator[...].astype(F32)

    def where_one(test):
        return jnp.where(test, 1.0, 0.0).astype(BF16)

    def grid_of(shape):
        return [lax.broadcasted_iota(jnp.int32, shape, i) for i in range(2)]

    r, c = grid_of((side, chan * phys))
    pick_row = where_one((r // (group * phys) == c // phys) & (r % phys == c % phys))
    r, c = grid_of((chan, side))
    total = jnp.zeros((side, side), F32)
    for t in range(phys):
        tall = jnp.dot(
            pick_row,
            lines[pl.ds(t, chan * phys, stride=phys), :].astype(BF16),
            preferred_element_type=F32,
        ).astype(BF16)
        pick_column = where_one((c // (group * chan) == t) & (c % chan == r))
        total = total + jnp.dot(tall, pick_column, preferred_element_type=F32)
    r, c = grid_of((side, side))
    same = (r // phys) % group == (c // chan) % group
    spread[...] = jnp.where(same, total, 0.0).astype(BF16)

    def prepare_right(n):
        pltpu.make_async_copy(right.at[n], right_in.at[n], right_sem.at[n]).wait()
        pitch = blk + PAD
        for w in range(chan):
            planes[w * pitch : w * pitch + blk, :] = right_in[n, w].astype(F32).T
        for b in range(blk):
            right_t[n, b * chan : (b + 1) * chan, :] = planes[
                pl.ds(b, chan, stride=pitch), :
            ].astype(BF16)

    def prepare_left(n):
        for u in range(chan):
            left_t[n, u * blk : (u + 1) * blk, :] = left_in[n, u].T

    def sum8(value):
        return jnp.sum(value.reshape(-1, 8, value.shape[-1]), axis=0)

    def operate(n, slot, vector, arrive):
        half = group * chan
        for j in range(blk // pair):
            rows = right_t[n, j * pair * chan : (j + 1) * pair * chan, :]
            first = jnp.dot(rows, vector, preferred_element_type=F32).astype(BF16)
            stacked = [
                jnp.concatenate(
                    [
                        first[g * half : (g + 1) * half, t * blk : (t + 1) * blk]
                        for t in range(phys)
                    ],
                    axis=0,
                )
                for g in range(2)
            ]
            second = jnp.dot(
                spread[...], jnp.concatenate(stacked, axis=1), preferred_element_type=F32
            ).astype(BF16)
            tile = group * phys
            for g in range(2):
                row = (2 * j + g) * tile
                for u in range(chan):
                    mixed[slot, row : row + tile, u * blk : (u + 1) * blk] = second[
                        u * tile : (u + 1) * tile, g * blk : (g + 1) * blk
                    ]
        arrive()
        rows_buf[slot] = jnp.dot(mixed[slot], left_t[n], preferred_element_type=F32)
        return [rows_buf[slot, pl.ds(s, blk, stride=phys), :] for s in range(phys)]

    def reduce(turn, sums):
        line = lax.broadcasted_iota(jnp.int32, (8, blk), 0)
        tile = jnp.zeros((8, blk), F32)
        for q, total in enumerate(sums):
            tile = jnp.where(line == q, jnp.sum(total, axis=0, keepdims=True), tile)
        part[turn] = tile
        gathered[turn, mine] = tile

        def copy_of(k, slot):
            return pltpu.make_async_remote_copy(
                src_ref=part.at[turn], dst_ref=gathered.at[turn, slot],
                send_sem=sum_send.at[turn, k - 1], recv_sem=sum_recv.at[turn, k - 1],
                device_id={"sector": lax.rem(mine + k, sectors)}, device_id_type=MESH,
            )

        for k in range(1, sectors):
            copy_of(k, mine).start()
        for k in range(1, sectors):
            copy_of(k, lax.rem(mine + sectors - k, sectors)).wait()
        total = gathered[turn, 0]
        for i in range(1, sectors):
            total = total + gathered[turn, i]
        total = jnp.broadcast_to(jnp.sum(total, axis=1, keepdims=True), (8, blk))
        return [total[q : q + 1] for q in range(len(sums))]

    zero = jnp.zeros((8, blk), F32)

    def open_slot(n, sums):
        prepare_right(n)
        alive = jnp.broadcast_to(jnp.where(n < live_slots, 1.0, 0.0), (1, blk)).astype(F32)
        pltpu.make_async_copy(start.at[n], start_in.at[n], start_sem.at[n]).wait()
        rows_buf[0] = start_in[n].astype(F32)
        firsts = []
        for t in range(phys):
            first = rows_buf[0, pl.ds(t, blk, stride=phys), :].T * alive
            current[n, t] = first
            firsts.append(first.astype(BF16))
        offset = shift[pl.ds(n, 1)]

        def arrive():
            @pl.when(me > 0)
            def _():
                left_copy(n).wait_recv()

            @pl.when(me == 0)
            def _():
                own_copy(n).wait()

            prepare_left(n)

        results = operate(n, 0, jnp.concatenate(firsts, axis=1), arrive)
        a, b, c = sums
        for s in range(phys):
            first = current[n, s]
            value = results[s] + offset * first
            applied[n, s] = value
            a, b, c = a + sum8(first * first), b + sum8(first * value), c + sum8(value * value)
        return a, b, c

    sums = lax.fori_loop(0, slots, open_slot, (zero, zero, zero))
    norm_sum, first_quotient, first_sq = reduce(0, sums)
    inverse = lax.rsqrt(norm_sum + EPS)
    quotient = first_quotient * inverse * inverse
    image_sq = first_sq * inverse * inverse
    weight = norm_sum / (norm_sum + EPS)
    cos_part = inverse
    sin_part = None
    for turn in range(DAV):
        resid_sq = image_sq - quotient * quotient * (2.0 - weight)
        factor = lax.rsqrt(resid_sq + EPS)

        def next_slot(n, sums, cos_part=cos_part, sin_part=sin_part, quotient=quotient, factor=factor):
            probes = []
            for t in range(phys):
                state, moved = cos_part * current[n, t], cos_part * applied[n, t]
                if sin_part is not None:
                    state = state + sin_part * search[n, t]
                    moved = moved + sin_part * image[n, t]
                current[n, t] = state
                applied[n, t] = moved
                probe = (moved - quotient * state) * factor
                search[n, t] = probe
                probes.append(probe.astype(BF16))
            results = operate(n, 0, jnp.concatenate(probes, axis=1), lambda: None)
            offset = shift[pl.ds(n, 1)]
            a, b, c = sums
            for s in range(phys):
                value = results[s] + offset * search[n, s].astype(BF16).astype(F32)
                image[n, s] = value
                a = a + sum8(current[n, s] * value)
                b = b + sum8(applied[n, s] * value)
                c = c + sum8(value * value)
            return a, b, c

        sums = lax.fori_loop(0, slots, next_slot, (zero, zero, zero))
        along_state, along_image, search_sq = reduce(turn + 1, sums)
        curvature = factor * (along_image - quotient * along_state)
        cos_part, sin_part = half_rotation(-2.0 * resid_sq * factor, curvature - quotient)
        cross_term = factor * (image_sq - quotient * quotient)
        inner_term = factor * quotient * (1.0 - weight)
        next_quotient = (
            cos_part * cos_part * quotient
            + cos_part * sin_part * (along_state + cross_term)
            + sin_part * sin_part * curvature
        )
        next_sq = (
            cos_part * cos_part * image_sq
            + 2.0 * cos_part * sin_part * along_image
            + sin_part * sin_part * search_sq
        )
        weight = (
            cos_part * cos_part * weight
            + 2.0 * cos_part * sin_part * inner_term
            + sin_part * sin_part * resid_sq * factor * factor
        )
        quotient, image_sq = next_quotient, next_sq

    energy_out[...] = jnp.broadcast_to(quotient, (8, blk))
    scale = math.sqrt(slots * sectors * blk * phys * blk)

    for n in range(slots):
        for t in range(phys):
            state = cos_part * current[n, t] + sin_part * search[n, t]
            state_out[n, t] = (scale * state).astype(BF16)

    @pl.when(me < regions - 1)
    def _():
        for n in range(slots):
            left_copy(n).wait_send()


def finish(state, energy, out, density, energy_out, rows_buf, out_buf, density_buf, sems):
    slots, phys, blk, _ = state.shape
    copies = []
    for n in range(slots):
        total = jnp.zeros((blk, blk), F32)
        for s in range(phys):
            turned = state[n, s].T
            rows_buf[n, pl.ds(s, blk, stride=phys), :] = turned.astype(F32)
            total = total + jnp.dot(turned, state[n, s], preferred_element_type=F32)
        out_buf[n] = rows_buf[n].astype(BF16)
        density_buf[n] = total / (phys * blk)
        for i, (src, dst) in enumerate(((out_buf, out), (density_buf, density))):
            copies.append(pltpu.make_async_copy(src.at[n], dst.at[n], sems.at[i, n]))
            copies[-1].start()
    energy_out[0] = energy[0, 0]
    for copy in copies:
        copy.wait()


def body(regions, sectors, start_state, left_env, right_env, mpo_tensor, decay, energy_terms, live_count):
    _, slots, blk, phys, _ = start_state.shape
    chan = left_env.shape[2]
    wide = phys * blk
    group = 256 // (phys * chan)
    vmem = pl.BlockSpec(memory_space=pltpu.VMEM)
    hbm = pl.BlockSpec(memory_space=pl.ANY)
    smem = pl.BlockSpec(memory_space=pltpu.SMEM)
    dma = pltpu.SemaphoreType.DMA
    state = pltpu.VMEM((slots, phys, blk, blk), F32)
    outs = pl.pallas_call(
        functools.partial(kernel, regions, sectors),
        out_shape=(
            jax.ShapeDtypeStruct((slots, phys, blk, blk), BF16),
            jax.ShapeDtypeStruct((8, blk), F32),
        ),
        in_specs=[hbm, hbm, hbm, vmem, vmem, vmem, vmem],
        out_specs=(vmem, vmem),
        scratch_shapes=[
            pltpu.VMEM((slots, wide, blk), BF16),
            pltpu.VMEM((slots, chan, blk, blk), BF16),
            pltpu.VMEM((slots, chan * blk, blk), BF16),
            pltpu.VMEM((slots, chan, blk, blk), BF16),
            pltpu.VMEM((slots, chan * blk, blk), BF16),
            pltpu.VMEM((chan * (blk + PAD), blk), F32),
            pltpu.VMEM((2, wide, blk), F32),
            pltpu.VMEM((2, wide, chan * blk), BF16),
            pltpu.VMEM((chan * phys * phys, chan), F32),
            pltpu.VMEM((group * phys * chan, group * phys * chan), BF16),
            state, state, state, state,
            pltpu.VMEM((regions, slots, blk), F32),
            pltpu.VMEM((regions, slots, blk), F32),
            pltpu.VMEM((slots, blk), F32),
            pltpu.VMEM((DAV + 1, 8, blk), F32),
            pltpu.VMEM((DAV + 1, sectors, 8, blk), F32),
            dma((slots,)), dma((slots,)), dma((slots,)), dma((slots,)), dma((slots,)),
            dma((2, regions)), dma((2, regions)),
            dma((DAV + 1, sectors)), dma((DAV + 1, sectors)),
        ],
        compiler_params=pltpu.CompilerParams(collective_id=0, has_side_effects=True),
    )(
        start_state.reshape(slots, wide, blk), left_env[0], right_env[0],
        mpo_tensor.reshape(chan * phys * phys, chan),
        decay[0], energy_terms[0], live_count,
    )
    state_out, density, energy = pl.pallas_call(
        finish,
        out_shape=(
            jax.ShapeDtypeStruct((slots, wide, blk), BF16),
            jax.ShapeDtypeStruct((slots, blk, blk), F32),
            jax.ShapeDtypeStruct((1,), F32),
        ),
        in_specs=[vmem, vmem],
        out_specs=(hbm, hbm, smem),
        scratch_shapes=[
            pltpu.VMEM((slots, wide, blk), F32),
            pltpu.VMEM((slots, wide, blk), BF16),
            pltpu.VMEM((slots, blk, blk), F32),
            dma((2, slots)),
        ],
    )(*outs)
    return (
        state_out.reshape(start_state.shape),
        density.reshape(1, slots, blk, blk),
        energy,
    )


def solution(mesh):
    in_specs = (
        P("region", "sector", None, None, None),
        P("region", "sector", None, None, None),
        P("region", "sector", None, None, None),
        P(),
        P("region", "sector", None),
        P("region", "sector", None),
        P("region", "sector"),
    )
    out_specs = (
        P("region", "sector", None, None, None),
        P("region", "sector", None, None),
        P("region"),
    )
    step = functools.partial(body, mesh.shape["region"], mesh.shape["sector"])
    return jax.shard_map(step, mesh=mesh, in_specs=in_specs, out_specs=out_specs, check_vma=False)
```
